1024 devices in a mesh: ctx: 16 (over x, y), head: 4 (over z_hi), dp: 16 (over z_lo, core).
Axes of the slice: x: 4, y: 4, z: 32 (z_hi: 4, z_lo: 8; z = z_hi * 8 + z_lo), core: 2. Of those that a mesh axis runs over, the one named last changes fastest.
Arguments:
- query_raw: bfloat16 [16, 2048, 4096], P('dp', 'ctx', 'head'), may hold values from -6 to 6
- key_raw: bfloat16 [16, 2048, 512], P('dp', 'ctx', 'head'), may hold values from -6 to 6
- value_rows: bfloat16 [16, 2048, 512], P('dp', 'ctx', 'head'), may hold values from -6 to 6
- attn_out: bfloat16 [16, 2048, 4096], P('dp', 'ctx', 'head'), may hold values from -2 to 2
- out_grad: bfloat16 [16, 2048, 4096], P('dp', 'ctx', 'head'), may hold values from -6 to 6
- log_totals: float32 [16, 32, 2048], P('dp', 'head', 'ctx'), may hold values from -40 to 40, as said below
- query_gain: float32 [128], replicated, may hold values from 0.5 to 1.5
- key_gain: float32 [128], replicated, may hold values from 0.5 to 1.5
Outputs:
- grad_query: float32 [16, 2048, 4096], P('dp', 'ctx', 'head')
- grad_key: float32 [16, 2048, 512], P('dp', 'ctx', 'head')
- grad_value: float32 [16, 2048, 512], P('dp', 'ctx', 'head')
- gain_grads: float32 [2, 128], replicated
The draws below stay inside these ranges and needn't reach their ends.
Inputs may be any that keep to these rules, and one draw needn't show every extreme that they name: log_totals[s, h, i] is the log of the sum over j <= i of exp(score[i, j]) for query head h, computed from query_raw, key_raw and the gains.
All inputs are finite; a program needn't handle non-finite values.
Results may differ from the reference program's by a relative error of at most 0.009.
Values may be sent and summed in bfloat16 or wider, within the bound.
No kernel may reach another device: no remote copies, remote signals or barrier semaphores. Data moves between devices by JAX's collectives and lax.ppermute only.
A program may use at most 32 MiB of HBM per device.

```python
import math
import jax
import jax.numpy as jnp
from jax import lax

HD = 128
HEADS = 32
KV_HEADS = 4
TOK_DEV = 128
LENGTH = 2048
SEQS = 16
N_CTX = 16


def shared_draw(key):
    query_shape = (SEQS, LENGTH, HEADS * HD)
    key_shape = (SEQS, LENGTH, KV_HEADS * HD)
    query_values = jnp.clip(jax.random.normal(jax.random.fold_in(key, 101), query_shape, jnp.float32), -5.5, 5.5)
    key_values = jnp.clip(jax.random.normal(jax.random.fold_in(key, 102), key_shape, jnp.float32), -5.5, 5.5)
    query_values = query_values.astype(jnp.bfloat16)
    key_values = key_values.astype(jnp.bfloat16)
    query_gain = jax.random.uniform(jax.random.fold_in(key, 103), (HD,), jnp.float32, 0.5, 1.5)
    key_gain = jax.random.uniform(jax.random.fold_in(key, 104), (HD,), jnp.float32, 0.5, 1.5)
    logit_scale = 1.0 / math.sqrt(HD)
    group = HEADS // KV_HEADS
    positions = jnp.arange(LENGTH)
    causal = positions[:, None] >= positions[None, :]

    def normed(raw_rows, norm_gain, count):
        values = raw_rows.astype(jnp.float32).reshape(LENGTH, count, HD)
        inverse = lax.rsqrt(jnp.mean(values * values, axis=-1, keepdims=True) + 1e-06)
        return (values * inverse * norm_gain).astype(jnp.bfloat16).astype(jnp.float32)

    def one_group(inputs):
        grouped_queries, grouped_keys = inputs
        attention_logits = jnp.einsum('gqd,kd->gqk', grouped_queries, grouped_keys) * logit_scale
        masked = jnp.where(causal[None], attention_logits, -jnp.inf)
        highest = jnp.max(masked, axis=-1, keepdims=True)
        return highest[:, :, 0] + jnp.log(jnp.sum(jnp.exp(masked - highest), axis=-1))

    def one_sequence(inputs):
        query_seq, key_seq = inputs
        q_groups = normed(query_seq, query_gain, HEADS).reshape(LENGTH, KV_HEADS, group, HD).transpose(1, 2, 0, 3)
        k_groups = normed(key_seq, key_gain, KV_HEADS).transpose(1, 0, 2)
        return lax.map(one_group, (q_groups, k_groups)).reshape(HEADS, LENGTH)
    totals = lax.map(one_sequence, (query_values, key_values))
    return (query_values, key_values, query_gain, key_gain, totals)


def draw_query_raw(key, part):
    return shared_draw(key)[0]


def draw_key_raw(key, part):
    return shared_draw(key)[1]


def draw_query_gain(key, part):
    return shared_draw(key)[2]


def draw_key_gain(key, part):
    return shared_draw(key)[3]


def draw_log_totals(key, part):
    return shared_draw(key)[4]


def block_levels(stream_key, extent, split, low, largest):
    def one(axis_at, blocks):
        steps = jax.random.uniform(jax.random.fold_in(jax.random.fold_in(stream_key, 6), axis_at), (blocks,), jnp.float32, low / len(split), largest / len(split))
        return jnp.repeat(jnp.exp(steps), extent[axis_at] // blocks).reshape((-1,) + (1,) * (len(extent) - axis_at - 1))

    level = one(*split[0])
    for cut in split[1:]:
        level = level * one(*cut)
    return level


def scatter_about(key, dims, scale, limit, pieces=(), held_as=jnp.bfloat16):
    level = block_levels(key, dims, pieces, -0.22, 0.18) if pieces else 1.0
    entries = jax.random.normal(key, dims, jnp.float32) * scale * level
    return jnp.minimum(jnp.maximum(entries, -limit), limit).astype(held_as)


def setup_inputs(seed: int = 0) -> dict:
    key_list = jax.random.split(jax.random.key(seed), 9)
    query_raw = draw_query_raw(jax.random.fold_in(key_list[8], 71), 0)
    key_raw = draw_key_raw(jax.random.fold_in(key_list[8], 71), 0)
    value_rows = scatter_about(key_list[2], (SEQS, LENGTH, KV_HEADS * HD), 1.0, 6.0, ((0, 16), (1, 16), (2, 4)))
    attn_out = scatter_about(key_list[3], (SEQS, LENGTH, HEADS * HD), 0.3, 2.0, ((0, 16), (1, 16), (2, 4)))
    out_grad = scatter_about(key_list[4], (SEQS, LENGTH, HEADS * HD), 1.0, 6.0, ((0, 16), (1, 16), (2, 4)))
    log_totals = draw_log_totals(jax.random.fold_in(key_list[8], 71), 0)
    query_gain = draw_query_gain(jax.random.fold_in(key_list[8], 71), 0)
    key_gain = draw_key_gain(jax.random.fold_in(key_list[8], 71), 0)
    return dict(query_raw=query_raw, key_raw=key_raw, value_rows=value_rows, attn_out=attn_out, out_grad=out_grad, log_totals=log_totals, query_gain=query_gain, key_gain=key_gain)


def normalize(raw_rows, norm_gain):
    values = raw_rows.astype(jnp.float32).reshape(raw_rows.shape[:-1] + (-1, HD))
    inverse = lax.rsqrt(lax.optimization_barrier(jnp.mean(values * values, axis=-1, keepdims=True)) + 1e-06)
    unit_rows = values * inverse
    return (unit_rows, inverse, (unit_rows * norm_gain).astype(jnp.bfloat16))

def norm_back(grad_norm, unit_rows, inverse, norm_gain):
    grad_unit = grad_norm * norm_gain
    grad_raw = (grad_unit - unit_rows * lax.optimization_barrier(jnp.mean(grad_unit * unit_rows, axis=-1, keepdims=True))) * inverse
    return (grad_raw, lax.optimization_barrier(jnp.sum(grad_norm * unit_rows, axis=(0, 1))))

def rounded_values(values):
    return lax.optimization_barrier(values.astype(jnp.bfloat16)).astype(jnp.float32)

def reference(query_raw, key_raw, value_rows, attn_out, out_grad, log_totals, query_gain, key_gain):
    blocks = N_CTX
    rows = TOK_DEV
    group = HEADS // KV_HEADS
    logit_scale = 1.0 / math.sqrt(HD)
    positions = jnp.arange(LENGTH).reshape(blocks, rows)
    causal = positions[:, :, None, None] >= positions[None, None, :, :]

    def one_group(inputs):
        grouped_queries, grouped_keys, grouped_values, output_grad_group, d_group, t_group = inputs
        attention_logits = jnp.einsum('vcow,ziw->ovczi', grouped_queries, grouped_keys) * logit_scale
        probs = jnp.where(causal[None], jnp.exp(attention_logits - t_group[:, :, :, None, None]), 0.0)
        probs_low = rounded_values(probs)
        value_parts = rounded_values(jnp.einsum('gaqbk,aqgd->abkd', probs_low, output_grad_group))
        grad_value = lax.optimization_barrier(jnp.sum(value_parts, axis=0)).reshape(LENGTH, HD)
        probability_gradient = jnp.einsum('vcow,ziw->ovczi', output_grad_group, grouped_values)
        score_gradient = rounded_values(probs * (probability_gradient - d_group.transpose(2, 0, 1)[:, :, :, None, None]))
        query_pieces = rounded_values(jnp.einsum('vlhsr,srn->lshvn', score_gradient, grouped_keys) * logit_scale)
        key_parts = rounded_values(jnp.einsum('gaqbk,aqgd->abkd', score_gradient, grouped_queries) * logit_scale)
        grad_q = lax.optimization_barrier(jnp.sum(query_pieces, axis=1)).reshape(LENGTH, group, HD)
        grad_k = lax.optimization_barrier(jnp.sum(key_parts, axis=0)).reshape(LENGTH, HD)
        return (grad_q, grad_k, grad_value)

    def one_sequence(inputs):
        query_seq, key_seq, value_seq, output_seq, grad_seq, totals_seq = inputs
        q_unit, q_inverse, q_norm = normalize(query_seq, query_gain)
        k_unit, k_inverse, k_norm = normalize(key_seq, key_gain)
        q_blocks = q_norm.astype(jnp.float32).reshape(blocks, rows, KV_HEADS, group, HD).transpose(2, 0, 1, 3, 4)
        g_blocks = grad_seq.astype(jnp.float32).reshape(blocks, rows, KV_HEADS, group, HD).transpose(2, 0, 1, 3, 4)
        o_blocks = output_seq.astype(jnp.float32).reshape(blocks, rows, KV_HEADS, group, HD).transpose(2, 0, 1, 3, 4)
        d_blocks = lax.optimization_barrier(jnp.sum(g_blocks * o_blocks, axis=-1))
        k_blocks = k_norm.astype(jnp.float32).reshape(blocks, rows, KV_HEADS, HD).transpose(2, 0, 1, 3)
        v_blocks = value_seq.astype(jnp.float32).reshape(blocks, rows, KV_HEADS, HD).transpose(2, 0, 1, 3)
        totals = totals_seq.reshape(KV_HEADS, group, blocks, rows)
        grad_q, grad_k, grad_v = lax.map(one_group, (q_blocks, k_blocks, v_blocks, g_blocks, d_blocks, totals))
        grad_q_norm = grad_q.transpose(1, 0, 2, 3).reshape(LENGTH, HEADS, HD)
        grad_k_norm = grad_k.transpose(1, 0, 2)
        grad_value = grad_v.transpose(1, 0, 2).reshape(LENGTH, KV_HEADS * HD)
        grad_query, q_gain_sum = norm_back(grad_q_norm, q_unit, q_inverse, query_gain)
        grad_key, k_gain_sum = norm_back(grad_k_norm, k_unit, k_inverse, key_gain)
        return (grad_query.reshape(LENGTH, HEADS * HD), grad_key.reshape(LENGTH, KV_HEADS * HD), grad_value, q_gain_sum, k_gain_sum)
    grad_query, grad_key, grad_value, q_sums, k_sums = lax.map(one_sequence, (query_raw, key_raw, value_rows, attn_out, out_grad, log_totals))
    factor = 1.0 / math.sqrt(SEQS * LENGTH * HEADS)
    gain_grads = jnp.stack([lax.optimization_barrier(jnp.sum(q_sums, axis=0)), lax.optimization_barrier(jnp.sum(k_sums, axis=0))]) * factor
    return (grad_query, grad_key, grad_value, gain_grads)
```

```python
import functools
import math

import jax
import jax.numpy as jnp
from jax import lax
from jax.experimental import pallas as pl
from jax.experimental.pallas import tpu as pltpu
from jax.sharding import PartitionSpec as P

HD = 128
TAIL = 8
EPS = 1e-06
LOG2E = 1.4426950408889634
F32 = jnp.float32
BF16 = jnp.bfloat16


def prologue(q_ref, o_ref, g_ref, lt_ref, qgain_ref, qn_ref, qt_ref, ut_ref, gs_ref, gt_ref, rows_ref):
    rows = q_ref.shape[0]
    for h in range(q_ref.shape[1] // HD):
        cols = slice(h * HD, (h + 1) * HD)
        span = slice(h * rows, (h + 1) * rows)
        q = q_ref[:, cols].astype(F32)
        inverse = lax.rsqrt(jnp.mean(q * q, axis=-1, keepdims=True) + EPS)
        unit = q * inverse
        ut_ref[:, span] = unit.T
        qn = (unit * qgain_ref[...]).astype(BF16)
        qn_ref[span, :] = qn
        qt_ref[:, span] = qn.astype(F32).T.astype(BF16)
        g = g_ref[:, cols]
        gs_ref[span, :] = g
        g_turned = g.astype(F32).T
        gt_ref[:, span] = g_turned.astype(BF16)
        o_turned = o_ref[:, cols].astype(F32).T
        rows_ref[0:1, span] = lt_ref[h : h + 1, :] * LOG2E
        rows_ref[1:2, span] = jnp.sum(g_turned * o_turned, axis=0, keepdims=True)


def attention(
    block_ref, kv_ref, qn_ref, qt_ref, ut_ref, gs_ref, gt_ref, rows_ref, kgain_ref,
    dqt_ref, parts_ref,
    kn_ref, kt_ref, unit_ref,
):
    blocks, rows = kv_ref.shape[0], kv_ref.shape[1]
    width = qt_ref.shape[1]
    scale = 1.0 / math.sqrt(HD)
    pair = 2 * rows
    wide = 2 * rows
    block = block_ref[0]
    last = block // 2
    for j in range(blocks // 2):
        k = kv_ref[2 * j : 2 * j + 2, :, :HD].reshape(pair, HD).astype(F32)
        inverse = lax.rsqrt(jnp.mean(k * k, axis=-1, keepdims=True) + EPS)
        unit = k * inverse
        kn = (unit * kgain_ref[...]).astype(BF16)
        unit_ref[j] = unit
        kn_ref[j] = kn
        kt_ref[j] = kn.astype(F32).T.astype(BF16)
    dqt_ref[...] = jnp.zeros(dqt_ref.shape, F32)

    def step(j, k_gain, masked):
        kn = kn_ref[j]
        kt = kt_ref[j]
        v = kv_ref[pl.ds(2 * j, 2), :, HD:].reshape(pair, HD)
        dk = jnp.zeros((pair, HD), F32)
        dv = jnp.zeros((pair, HD), F32)
        if masked:
            key_pos = j * pair + lax.broadcasted_iota(jnp.int32, (pair, wide), 0)
            query_pos = block * rows + lax.broadcasted_iota(jnp.int32, (pair, wide), 1) % rows
            keep = key_pos <= query_pos
        for c in range(width // wide):
            span = slice(c * wide, (c + 1) * wide)
            scores = jnp.dot(kn, qt_ref[:, span], preferred_element_type=F32)
            probs = jnp.exp2(scores * (scale * LOG2E) - rows_ref[0:1, span])
            if masked:
                probs = jnp.where(keep, probs, 0.0)
            dv += jnp.dot(probs.astype(BF16), gs_ref[span, :], preferred_element_type=F32)
            dp = jnp.dot(v, gt_ref[:, span], preferred_element_type=F32)
            ds = (probs * (dp - rows_ref[1:2, span])).astype(BF16)
            dk += jnp.dot(ds, qn_ref[span, :], preferred_element_type=F32)
            dqt_ref[:, span] += jnp.dot(kt, ds, preferred_element_type=F32)
        dk = dk * scale
        parts_ref[pl.ds(2 * j, 2), :rows, :HD] = dk.astype(BF16).reshape(2, rows, HD)
        parts_ref[pl.ds(2 * j, 2), :rows, HD:] = dv.astype(BF16).reshape(2, rows, HD)
        return k_gain + jnp.sum(dk * unit_ref[j], axis=0, keepdims=True)

    k_gain = lax.fori_loop(0, last, lambda j, s: step(j, s, False), jnp.zeros((1, HD), F32))
    k_gain = step(last, k_gain, True)

    def clear(j, carry):
        parts_ref[pl.ds(2 * j, 2), :rows] = jnp.zeros((2, rows, 2 * HD), BF16)
        return carry

    lax.fori_loop(last + 1, blocks // 2, clear, 0)
    product = jnp.zeros((HD, wide), F32)
    for c in range(width // wide):
        span = slice(c * wide, (c + 1) * wide)
        product += dqt_ref[:, span] * ut_ref[:, span]
    q_gain = jnp.sum((product[:, :HD] + product[:, HD:]).T, axis=0, keepdims=True) * scale
    sums = jnp.concatenate([q_gain, k_gain], axis=1)
    high = sums.astype(BF16).astype(F32)
    middle = (sums - high).astype(BF16).astype(F32)
    low = sums - high - middle
    tail = jnp.concatenate([high, middle, low, jnp.zeros((TAIL - 3, 2 * HD), F32)], axis=0)
    tail = tail.astype(BF16)
    for b in range(blocks):
        parts_ref[b, rows:] = tail


def query_end(dqt_ref, q_ref, qgain_ref, gq_ref):
    rows = q_ref.shape[0]
    scale = 1.0 / math.sqrt(HD)
    for h in range(q_ref.shape[1] // HD):
        cols = slice(h * HD, (h + 1) * HD)
        grad_norm = dqt_ref[:, h * rows : (h + 1) * rows].T * scale
        q = q_ref[:, cols].astype(F32)
        inverse = lax.rsqrt(jnp.mean(q * q, axis=-1, keepdims=True) + EPS)
        unit = q * inverse
        grad_unit = grad_norm * qgain_ref[...]
        mean = jnp.mean(grad_unit * unit, axis=-1, keepdims=True)
        gq_ref[:, cols] = (grad_unit - unit * mean) * inverse


def near_sum(parts_ref, gains_ref):
    total = parts_ref[0, -TAIL:].astype(F32)
    for b in range(1, parts_ref.shape[0]):
        total += parts_ref[b, -TAIL:].astype(F32)
    sums = jnp.sum(total, axis=0, keepdims=True)
    sums = jnp.concatenate([sums[:, :HD], sums[:, HD:]], axis=0)
    for i in range(gains_ref.shape[0]):
        gains_ref[i] = sums


def far_sum(gains_ref, out_ref, *, factor):
    out_ref[...] = jnp.sum(gains_ref[...], axis=0) * factor


def key_end(parts_ref, k_ref, kgain_ref, gk_ref, gv_ref):
    rows = k_ref.shape[0]
    total = parts_ref[0, :rows].astype(F32)
    for b in range(1, parts_ref.shape[0]):
        total += parts_ref[b, :rows].astype(F32)
    grad_norm = total[:, :HD]
    gv_ref[...] = total[:, HD:]
    k = k_ref[...].astype(F32)
    inverse = lax.rsqrt(jnp.mean(k * k, axis=-1, keepdims=True) + EPS)
    unit = k * inverse
    grad_unit = grad_norm * kgain_ref[...]
    mean = jnp.mean(grad_unit * unit, axis=-1, keepdims=True)
    gk_ref[...] = (grad_unit - unit * mean) * inverse


def spread_rows(k_ref, v_ref, out_ref):
    both = jnp.concatenate([k_ref[...], v_ref[...]], axis=1)
    for b in range(out_ref.shape[0]):
        out_ref[b] = both


def local(query_raw, key_raw, value_rows, attn_out, out_grad, log_totals, query_gain, key_gain):
    blocks = lax.axis_size("ctx")
    rows, width = query_raw.shape[1], query_raw.shape[2]
    heads = width // HD
    others = lax.axis_size("head") * lax.axis_size("dp")
    shape = jax.ShapeDtypeStruct
    query_gain = query_gain.reshape(1, HD)
    key_gain = key_gain.reshape(1, HD)
    spread = pl.pallas_call(
        spread_rows, out_shape=shape((blocks, rows, 2 * HD), BF16), name="spread_rows"
    )(key_raw[0], value_rows[0])
    gathered = lax.all_to_all(spread, "ctx", 0, 0, tiled=True)
    prepared = pl.pallas_call(
        prologue,
        out_shape=(
            shape((heads * rows, HD), BF16),
            shape((HD, heads * rows), BF16),
            shape((HD, heads * rows), F32),
            shape((heads * rows, HD), BF16),
            shape((HD, heads * rows), BF16),
            shape((2, heads * rows), F32),
        ),
        name="prologue",
    )(query_raw[0], attn_out[0], out_grad[0], log_totals[0], query_gain)
    in_vmem = pl.BlockSpec(memory_space=pltpu.VMEM)
    dqt, parts = pl.pallas_call(
        attention,
        out_shape=(shape((HD, heads * rows), F32), shape((blocks, rows + TAIL, 2 * HD), BF16)),
        in_specs=[pl.BlockSpec(memory_space=pltpu.SMEM)] + [in_vmem] * 8,
        scratch_shapes=[
            pltpu.VMEM((blocks // 2, 2 * rows, HD), BF16),
            pltpu.VMEM((blocks // 2, HD, 2 * rows), BF16),
            pltpu.VMEM((blocks // 2, 2 * rows, HD), F32),
        ],
        name="attention",
    )(lax.axis_index("ctx").reshape(1).astype(jnp.int32), gathered, *prepared, key_gain)
    returned = lax.all_to_all(parts, "ctx", 0, 0, tiled=True)
    grad_query = pl.pallas_call(
        query_end, out_shape=shape((rows, width), F32), name="query_end"
    )(dqt, query_raw[0], query_gain)
    gains = pl.pallas_call(
        near_sum, out_shape=shape((others, 2, HD), F32), name="near_sum"
    )(returned)
    gains = lax.all_to_all(gains, ("head", "dp"), 0, 0, tiled=True)
    grad_key, grad_value = pl.pallas_call(
        key_end,
        out_shape=(shape((rows, HD), F32), shape((rows, HD), F32)),
        name="key_end",
    )(returned, key_raw[0], key_gain)
    pair_count = query_raw.shape[0] * rows * blocks * heads * others
    gains = pl.pallas_call(
        functools.partial(far_sum, factor=1.0 / math.sqrt(pair_count)),
        out_shape=shape((2, HD), F32),
        name="far_sum",
    )(gains)
    return (grad_query[None], grad_key[None], grad_value[None], gains)


def solution(mesh):
    return jax.shard_map(
        local,
        mesh=mesh,
        in_specs=(
            P("dp", "ctx", "head"),
            P("dp", "ctx", "head"),
            P("dp", "ctx", "head"),
            P("dp", "ctx", "head"),
            P("dp", "ctx", "head"),
            P("dp", "head", "ctx"),
            P(),
            P(),
        ),
        out_specs=(P("dp", "ctx", "head"), P("dp", "ctx", "head"), P("dp", "ctx", "head"), P()),
        check_vma=False,
    )
```

```python
import functools
import math

import jax
import jax.numpy as jnp
from jax import lax
from jax.experimental import pallas as pl
from jax.experimental.pallas import tpu as pltpu
from jax.sharding import PartitionSpec as P

HD = 128
TAIL = 8
VMEM_LIMIT = 32 * 2**20
CTX_FIRST = 10
FAR_FIRST = 40
EPS = 1e-06
LOG2E = 1.4426950408889634
F32 = jnp.float32
BF16 = jnp.bfloat16


def prologue(q_ref, o_ref, g_ref, lt_ref, qgain_ref, qn_ref, qt_ref, ut_ref, gs_ref, gt_ref, rows_ref):
    rows = q_ref.shape[0]
    for h in range(q_ref.shape[1] // HD):
        cols = slice(h * HD, (h + 1) * HD)
        span = slice(h * rows, (h + 1) * rows)
        q = q_ref[:, cols].astype(F32)
        inverse = lax.rsqrt(jnp.mean(q * q, axis=-1, keepdims=True) + EPS)
        unit = q * inverse
        ut_ref[:, span] = unit.T
        qn = (unit * qgain_ref[...]).astype(BF16)
        qn_ref[span, :] = qn
        qt_ref[:, span] = qn.astype(F32).T.astype(BF16)
        g = g_ref[:, cols]
        gs_ref[span, :] = g
        g_turned = g.astype(F32).T
        gt_ref[:, span] = g_turned.astype(BF16)
        o_turned = o_ref[:, cols].astype(F32).T
        rows_ref[0:1, span] = lt_ref[h : h + 1, :] * LOG2E
        rows_ref[1:2, span] = jnp.sum(g_turned * o_turned, axis=0, keepdims=True)


def attention(
    block_ref, kv_ref, qn_ref, qt_ref, ut_ref, gs_ref, gt_ref, rows_ref, kgain_ref,
    dqt_ref, parts_ref,
    kn_ref, kt_ref, unit_ref,
):
    blocks, rows = kv_ref.shape[0], kv_ref.shape[1]
    width = qt_ref.shape[1]
    scale = 1.0 / math.sqrt(HD)
    pair = 2 * rows
    wide = 2 * rows
    block = block_ref[0]
    last = block // 2
    turn = blocks // 2 - CTX_FIRST % blocks // 2
    for j in range(blocks // 2):
        k = kv_ref[2 * j : 2 * j + 2, :, :HD].reshape(pair, HD).astype(F32)
        inverse = lax.rsqrt(jnp.mean(k * k, axis=-1, keepdims=True) + EPS)
        unit = k * inverse
        kn = (unit * kgain_ref[...]).astype(BF16)
        unit_ref[j] = unit
        kn_ref[j] = kn
        kt_ref[j] = kn.astype(F32).T.astype(BF16)
    dqt_ref[...] = jnp.zeros(dqt_ref.shape, F32)

    def step(j, k_gain, masked):
        at = (j + turn) % (blocks // 2)
        kn = kn_ref[at]
        kt = kt_ref[at]
        v = kv_ref[pl.ds(2 * at, 2), :, HD:].reshape(pair, HD)
        dk = jnp.zeros((pair, HD), F32)
        dv = jnp.zeros((pair, HD), F32)
        if masked:
            key_pos = j * pair + lax.broadcasted_iota(jnp.int32, (pair, wide), 0)
            query_pos = block * rows + lax.broadcasted_iota(jnp.int32, (pair, wide), 1) % rows
            keep = key_pos <= query_pos
        for c in range(width // wide):
            span = slice(c * wide, (c + 1) * wide)
            scores = jnp.dot(kn, qt_ref[:, span], preferred_element_type=F32)
            probs = jnp.exp2(scores * (scale * LOG2E) - rows_ref[0:1, span])
            if masked:
                probs = jnp.where(keep, probs, 0.0)
            dv += jnp.dot(probs.astype(BF16), gs_ref[span, :], preferred_element_type=F32)
            dp = jnp.dot(v, gt_ref[:, span], preferred_element_type=F32)
            ds = (probs * (dp - rows_ref[1:2, span])).astype(BF16)
            dk += jnp.dot(ds, qn_ref[span, :], preferred_element_type=F32)
            dqt_ref[:, span] += jnp.dot(kt, ds, preferred_element_type=F32)
        dk = dk * scale
        parts_ref[pl.ds(2 * at, 2), :rows, :HD] = dk.astype(BF16).reshape(2, rows, HD)
        parts_ref[pl.ds(2 * at, 2), :rows, HD:] = dv.astype(BF16).reshape(2, rows, HD)
        return k_gain + jnp.sum(dk * unit_ref[at], axis=0, keepdims=True)

    k_gain = lax.fori_loop(0, last, lambda j, s: step(j, s, False), jnp.zeros((1, HD), F32))
    k_gain = step(last, k_gain, True)

    def clear(j, carry):
        at = (j + turn) % (blocks // 2)
        parts_ref[pl.ds(2 * at, 2), :rows] = jnp.zeros((2, rows, 2 * HD), BF16)
        return carry

    lax.fori_loop(last + 1, blocks // 2, clear, 0)
    product = jnp.zeros((HD, wide), F32)
    for c in range(width // wide):
        span = slice(c * wide, (c + 1) * wide)
        product += dqt_ref[:, span] * ut_ref[:, span]
    q_gain = jnp.sum((product[:, :HD] + product[:, HD:]).T, axis=0, keepdims=True) * scale
    sums = jnp.concatenate([q_gain, k_gain], axis=1)
    high = sums.astype(BF16).astype(F32)
    middle = (sums - high).astype(BF16).astype(F32)
    low = sums - high - middle
    tail = jnp.concatenate([high, middle, low, jnp.zeros((TAIL - 3, 2 * HD), F32)], axis=0)
    tail = tail.astype(BF16)
    for b in range(blocks):
        parts_ref[b, rows:] = tail


def query_end(dqt_ref, q_ref, qgain_ref, gq_ref):
    rows = q_ref.shape[0]
    scale = 1.0 / math.sqrt(HD)
    for h in range(q_ref.shape[1] // HD):
        cols = slice(h * HD, (h + 1) * HD)
        grad_norm = dqt_ref[:, h * rows : (h + 1) * rows].T * scale
        q = q_ref[:, cols].astype(F32)
        inverse = lax.rsqrt(jnp.mean(q * q, axis=-1, keepdims=True) + EPS)
        unit = q * inverse
        grad_unit = grad_norm * qgain_ref[...]
        mean = jnp.mean(grad_unit * unit, axis=-1, keepdims=True)
        gq_ref[:, cols] = (grad_unit - unit * mean) * inverse


def near_sum(parts_ref, gains_ref):
    total = parts_ref[0, -TAIL:].astype(F32)
    for b in range(1, parts_ref.shape[0]):
        total += parts_ref[b, -TAIL:].astype(F32)
    sums = jnp.sum(total, axis=0, keepdims=True)
    sums = jnp.concatenate([sums[:, :HD], sums[:, HD:]], axis=0).astype(BF16)
    for i in range(gains_ref.shape[0]):
        gains_ref[i] = sums


def far_sum(gains_ref, out_ref, *, factor):
    out_ref[...] = jnp.sum(gains_ref[...].astype(F32), axis=0) * factor


def key_end(parts_ref, k_ref, kgain_ref, gk_ref, gv_ref):
    rows = k_ref.shape[0]
    total = parts_ref[0, :rows].astype(F32)
    for b in range(1, parts_ref.shape[0]):
        total += parts_ref[b, :rows].astype(F32)
    grad_norm = total[:, :HD]
    gv_ref[...] = total[:, HD:]
    k = k_ref[...].astype(F32)
    inverse = lax.rsqrt(jnp.mean(k * k, axis=-1, keepdims=True) + EPS)
    unit = k * inverse
    grad_unit = grad_norm * kgain_ref[...]
    mean = jnp.mean(grad_unit * unit, axis=-1, keepdims=True)
    gk_ref[...] = (grad_unit - unit * mean) * inverse


def spread_rows(k_ref, v_ref, out_ref):
    both = jnp.concatenate([k_ref[...], v_ref[...]], axis=1)
    for b in range(out_ref.shape[0]):
        out_ref[b] = both


def local_memory(values):
    return pltpu.with_memory_space_constraint(values, pltpu.VMEM)


def exchange(values, axes, count, first):
    order = [[(first + i) % count for i in range(count)]]
    return lax.all_to_all(values, axes, 0, 0, axis_index_groups=order, tiled=True)


def local(query_raw, key_raw, value_rows, attn_out, out_grad, log_totals, query_gain, key_gain):
    blocks = lax.axis_size("ctx")
    rows, width = query_raw.shape[1], query_raw.shape[2]
    heads = width // HD
    others = lax.axis_size("head") * lax.axis_size("dp")
    shape = jax.ShapeDtypeStruct
    near = pltpu.VMEM
    params = pltpu.CompilerParams(vmem_limit_bytes=VMEM_LIMIT)
    in_vmem = pl.BlockSpec(memory_space=pltpu.VMEM)
    query_gain = query_gain.reshape(1, HD)
    key_gain = key_gain.reshape(1, HD)
    spread = pl.pallas_call(
        spread_rows, out_shape=near((blocks, rows, 2 * HD), BF16), name="spread_rows", compiler_params=params
    )(key_raw[0], value_rows[0])
    gathered = exchange(spread, "ctx", blocks, CTX_FIRST)
    prepared = pl.pallas_call(
        prologue,
        out_shape=(
            near((heads * rows, HD), BF16),
            near((HD, heads * rows), BF16),
            near((HD, heads * rows), F32),
            near((heads * rows, HD), BF16),
            near((HD, heads * rows), BF16),
            near((2, heads * rows), F32),
        ),
        name="prologue", compiler_params=params,
    )(query_raw[0], attn_out[0], out_grad[0], log_totals[0], query_gain)
    dqt, parts = pl.pallas_call(
        attention,
        out_shape=(
            near((HD, heads * rows), F32),
            near((blocks, rows + TAIL, 2 * HD), BF16),
        ),
        in_specs=[pl.BlockSpec(memory_space=pltpu.SMEM)] + [in_vmem] * 8,
        scratch_shapes=[
            pltpu.VMEM((blocks // 2, 2 * rows, HD), BF16),
            pltpu.VMEM((blocks // 2, HD, 2 * rows), BF16),
            pltpu.VMEM((blocks // 2, 2 * rows, HD), F32),
        ],
        name="attention", compiler_params=params,
    )(lax.axis_index("ctx").reshape(1).astype(jnp.int32), local_memory(gathered), *prepared, key_gain)
    returned = exchange(parts, "ctx", blocks, CTX_FIRST)
    grad_query = pl.pallas_call(
        query_end, out_shape=shape((rows, width), F32), name="query_end", compiler_params=params
    )(dqt, query_raw[0], query_gain)
    gains = pl.pallas_call(
        near_sum, out_shape=near((others, 2, HD), BF16), name="near_sum", compiler_params=params
    )(local_memory(returned))
    gains = exchange(gains, ("head", "dp"), others, FAR_FIRST)
    grad_key, grad_value = pl.pallas_call(
        key_end,
        out_shape=(shape((rows, HD), F32), shape((rows, HD), F32)),
        name="key_end", compiler_params=params,
    )(local_memory(returned), key_raw[0], key_gain)
    pair_count = query_raw.shape[0] * rows * blocks * heads * others
    gains = pl.pallas_call(
        functools.partial(far_sum, factor=1.0 / math.sqrt(pair_count)),
        out_shape=shape((2, HD), F32),
        name="far_sum", compiler_params=params,
    )(local_memory(gains))
    return (grad_query[None], grad_key[None], grad_value[None], gains)


def solution(mesh):
    return jax.shard_map(
        local,
        mesh=mesh,
        in_specs=(
            P("dp", "ctx", "head"),
            P("dp", "ctx", "head"),
            P("dp", "ctx", "head"),
            P("dp", "ctx", "head"),
            P("dp", "ctx", "head"),
            P("dp", "head", "ctx"),
            P(),
            P(),
        ),
        out_specs=(P("dp", "ctx", "head"), P("dp", "ctx", "head"), P("dp", "ctx", "head"), P()),
        check_vma=False,
    )
```

```python
import functools
import math

import jax
import jax.numpy as jnp
from jax import lax
from jax.experimental import pallas as pl
from jax.experimental.pallas import tpu as pltpu
from jax.sharding import PartitionSpec as P

HD = 128
TAIL = 8
VMEM_LIMIT = 32 * 2**20
GATHER_FIRST = 10
GATHER_TURN = 3
BACK_FIRST = 14
BACK_TURN = 1
KEY_BLOCKS = 4
AHEAD = 1
Q_ROWS = 512
FAR_FIRST = 40
EPS = 1e-06
LOG2E = 1.4426950408889634
F32 = jnp.float32
BF16 = jnp.bfloat16


def prologue(q_ref, o_ref, g_ref, lt_ref, qgain_ref, qn_ref, qt_ref, un_ref, gt_ref, lse_ref, delta_ref):
    rows = q_ref.shape[0]
    for h in range(q_ref.shape[1] // HD):
        cols = slice(h * HD, (h + 1) * HD)
        span = slice(h * rows, (h + 1) * rows)
        q = q_ref[:, cols].astype(F32)
        inverse = lax.rsqrt(jnp.mean(q * q, axis=-1, keepdims=True) + EPS)
        unit = q * inverse
        un_ref[span, :] = unit
        qn = (unit * qgain_ref[...]).astype(BF16)
        qn_ref[span, :] = qn
        qt_ref[:, span] = qn.astype(F32).T.astype(BF16)
        g = g_ref[:, cols].astype(F32)
        gt_ref[:, span] = g.T.astype(BF16)
        delta = jnp.sum(g * o_ref[:, cols].astype(F32), axis=-1, keepdims=True)
        delta_ref[span, :] = jnp.broadcast_to(delta, (rows, HD))
        lse_ref[span, :] = jnp.broadcast_to(lt_ref[h : h + 1, :] * LOG2E, (HD, rows)).T


def attention(
    block_ref, kv_ref, qn_ref, qt_ref, un_ref, gt_ref, lse_ref, delta_ref, g_ref, kgain_ref,
    dq_ref, parts_ref,
    kn_ref, kt_ref, vt_ref, unit_ref,
):
    blocks, rows = kv_ref.shape[0], kv_ref.shape[1]
    width = qt_ref.shape[1]
    scale = 1.0 / math.sqrt(HD)
    pair = KEY_BLOCKS * rows
    twos = KEY_BLOCKS // 2
    wide = Q_ROWS
    block = block_ref[0]
    last = block // KEY_BLOCKS

    def prepare(j):
        ats = [(j * twos + i + GATHER_TURN) % (blocks // 2) for i in range(twos)]
        kv = [kv_ref[pl.ds(2 * at, 2)].reshape(2 * rows, 2 * HD) for at in ats]
        kv = jnp.concatenate(kv, axis=0).astype(F32)
        k = kv[:, :HD]
        v = kv[:, HD:]
        inverse = lax.rsqrt(jnp.mean(k * k, axis=-1, keepdims=True) + EPS)
        unit = k * inverse
        kn = (unit * kgain_ref[...]).astype(BF16)
        slot = j % 2
        unit_ref[slot] = unit
        kn_ref[slot] = kn
        kt_ref[slot] = kn.astype(F32).T.astype(BF16)
        vt_ref[slot] = v.T.astype(BF16)

    def step(j, k_gain, masked):
        slot = j % 2
        kn = kn_ref[slot]
        kt = kt_ref[slot]
        vt = vt_ref[slot]
        unit = unit_ref[slot]
        dkt = jnp.zeros((HD, pair), F32)
        dvt = jnp.zeros((HD, pair), F32)
        if masked:
            key_pos = j * pair + lax.broadcasted_iota(jnp.int32, (wide, pair), 1)
            query_pos = block * rows + lax.broadcasted_iota(jnp.int32, (wide, pair), 0) % rows
            keep = key_pos <= query_pos
        chunks = width // wide
        spans = [slice(c * wide, (c + 1) * wide) for c in range(chunks)]
        across = pair // HD

        def products(c):
            heads = range(c * wide // rows, (c + 1) * wide // rows)
            g = jnp.concatenate([g_ref[:, h * HD : (h + 1) * HD] for h in heads], axis=0)
            scores = jnp.dot(qn_ref[spans[c], :], kt, preferred_element_type=F32)
            return scores, jnp.dot(g, vt, preferred_element_type=F32)

        def weights(c, scores, dp):
            lse = jnp.concatenate([lse_ref[spans[c], :]] * across, axis=1)
            delta = jnp.concatenate([delta_ref[spans[c], :]] * across, axis=1)
            probs = jnp.exp2(scores * (scale * LOG2E) - lse)
            if masked:
                probs = jnp.where(keep, probs, 0.0)
            return probs.astype(BF16), (probs * (dp - delta)).astype(BF16)

        ahead = [products(c) for c in range(AHEAD)]
        for c in range(chunks):
            if c + AHEAD < chunks:
                ahead.append(products(c + AHEAD))
            low, ds = weights(c, *ahead[c])
            dvt += jnp.dot(gt_ref[:, spans[c]], low, preferred_element_type=F32)
            dkt += jnp.dot(qt_ref[:, spans[c]], ds, preferred_element_type=F32)
            dq_ref[spans[c], :] += jnp.dot(ds, kn, preferred_element_type=F32)
        dk = dkt.T * scale
        dv = dvt.T
        for i in range(twos):
            at = (j * twos + i + BACK_TURN) % (blocks // 2)
            piece = slice(2 * i * rows, 2 * (i + 1) * rows)
            parts_ref[pl.ds(2 * at, 2), :rows, :HD] = dk[piece].astype(BF16).reshape(2, rows, HD)
            parts_ref[pl.ds(2 * at, 2), :rows, HD:] = dv[piece].astype(BF16).reshape(2, rows, HD)
        if not masked:
            prepare(j + 1)
        return k_gain + jnp.sum(dk * unit, axis=0, keepdims=True)

    prepare(0)
    dq_ref[...] = jnp.zeros(dq_ref.shape, F32)
    k_gain = lax.fori_loop(0, last, lambda j, s: step(j, s, False), jnp.zeros((1, HD), F32))
    k_gain = step(last, k_gain, True)

    def clear(j, carry):
        at = (j + BACK_TURN) % (blocks // 2)
        parts_ref[pl.ds(2 * at, 2), :rows] = jnp.zeros((2, rows, 2 * HD), BF16)
        return carry

    lax.fori_loop((last + 1) * twos, blocks // 2, clear, 0)
    product = jnp.zeros((rows, HD), F32)
    for h in range(width // rows):
        span = slice(h * rows, (h + 1) * rows)
        product += dq_ref[span, :] * un_ref[span, :]
    q_gain = jnp.sum(product, axis=0, keepdims=True) * scale
    sums = jnp.concatenate([q_gain, k_gain], axis=1)
    high = sums.astype(BF16).astype(F32)
    middle = (sums - high).astype(BF16).astype(F32)
    low = sums - high - middle
    tail = jnp.concatenate([high, middle, low, jnp.zeros((TAIL - 3, 2 * HD), F32)], axis=0)
    tail = tail.astype(BF16)
    for b in range(blocks):
        parts_ref[b, rows:] = tail


def query_end(dq_ref, q_ref, qgain_ref, gq_ref):
    rows = q_ref.shape[0]
    scale = 1.0 / math.sqrt(HD)
    for h in range(q_ref.shape[1] // HD):
        cols = slice(h * HD, (h + 1) * HD)
        grad_norm = dq_ref[h * rows : (h + 1) * rows, :] * scale
        q = q_ref[:, cols].astype(F32)
        inverse = lax.rsqrt(jnp.mean(q * q, axis=-1, keepdims=True) + EPS)
        unit = q * inverse
        grad_unit = grad_norm * qgain_ref[...]
        mean = jnp.mean(grad_unit * unit, axis=-1, keepdims=True)
        gq_ref[:, cols] = (grad_unit - unit * mean) * inverse


def near_sum(parts_ref, gains_ref):
    total = parts_ref[0, -TAIL:].astype(F32)
    for b in range(1, parts_ref.shape[0]):
        total += parts_ref[b, -TAIL:].astype(F32)
    sums = jnp.sum(total, axis=0, keepdims=True)
    sums = jnp.concatenate([sums[:, :HD], sums[:, HD:]], axis=0).astype(BF16)
    for i in range(gains_ref.shape[0]):
        gains_ref[i] = sums


def far_sum(gains_ref, out_ref, *, factor):
    out_ref[...] = jnp.sum(gains_ref[...].astype(F32), axis=0) * factor


def key_end(parts_ref, k_ref, kgain_ref, gk_ref, gv_ref):
    rows = k_ref.shape[0]
    total = parts_ref[0, :rows].astype(F32)
    for b in range(1, parts_ref.shape[0]):
        total += parts_ref[b, :rows].astype(F32)
    grad_norm = total[:, :HD]
    gv_ref[...] = total[:, HD:]
    k = k_ref[...].astype(F32)
    inverse = lax.rsqrt(jnp.mean(k * k, axis=-1, keepdims=True) + EPS)
    unit = k * inverse
    grad_unit = grad_norm * kgain_ref[...]
    mean = jnp.mean(grad_unit * unit, axis=-1, keepdims=True)
    gk_ref[...] = (grad_unit - unit * mean) * inverse


def spread_rows(k_ref, v_ref, out_ref, both_ref, in_sem, out_sem):
    halves = (slice(0, HD), slice(HD, 2 * HD))
    ins = [
        pltpu.make_async_copy(ref, both_ref.at[:, half], in_sem.at[i])
        for i, (ref, half) in enumerate(zip((k_ref, v_ref), halves))
    ]
    for copy in ins:
        copy.start()
    for copy in ins:
        copy.wait()
    outs = [
        pltpu.make_async_copy(both_ref, out_ref.at[b], out_sem.at[b])
        for b in range(out_ref.shape[0])
    ]
    for copy in outs:
        copy.start()
    for copy in outs:
        copy.wait()


def local_memory(values):
    return pltpu.with_memory_space_constraint(values, pltpu.VMEM)


def far_memory(values):
    return pltpu.with_memory_space_constraint(values, pltpu.HBM)


def exchange(values, axes, count, first):
    order = [[(first + i) % count for i in range(count)]]
    return lax.all_to_all(values, axes, 0, 0, axis_index_groups=order, tiled=True)


def local(query_raw, key_raw, value_rows, attn_out, out_grad, log_totals, query_gain, key_gain):
    blocks = lax.axis_size("ctx")
    rows, width = query_raw.shape[1], query_raw.shape[2]
    heads = width // HD
    others = lax.axis_size("head") * lax.axis_size("dp")
    shape = jax.ShapeDtypeStruct
    near = pltpu.VMEM
    params = pltpu.CompilerParams(vmem_limit_bytes=VMEM_LIMIT)
    in_vmem = pl.BlockSpec(memory_space=pltpu.VMEM)
    query_gain = query_gain.reshape(1, HD)
    key_gain = key_gain.reshape(1, HD)
    in_hbm = pl.BlockSpec(memory_space=pltpu.HBM)
    spread = pl.pallas_call(
        spread_rows,
        in_specs=[in_hbm, in_hbm],
        out_specs=in_hbm,
        out_shape=shape((blocks, rows, 2 * HD), BF16),
        scratch_shapes=[
            pltpu.VMEM((rows, 2 * HD), BF16),
            pltpu.SemaphoreType.DMA((2,)),
            pltpu.SemaphoreType.DMA((blocks,)),
        ],
        name="spread_rows",
        compiler_params=params,
    )(far_memory(key_raw[0]), far_memory(value_rows[0]))
    gathered = exchange(spread, "ctx", blocks, GATHER_FIRST)
    prepared = pl.pallas_call(
        prologue,
        out_shape=(
            near((heads * rows, HD), BF16),
            near((HD, heads * rows), BF16),
            near((heads * rows, HD), F32),
            near((HD, heads * rows), BF16),
            near((heads * rows, HD), F32),
            near((heads * rows, HD), F32),
        ),
        name="prologue", compiler_params=params,
    )(query_raw[0], attn_out[0], out_grad[0], log_totals[0], query_gain)
    dq, parts = pl.pallas_call(
        attention,
        out_shape=(near((heads * rows, HD), F32), near((blocks, rows + TAIL, 2 * HD), BF16)),
        in_specs=[pl.BlockSpec(memory_space=pltpu.SMEM)] + [in_vmem] * 9,
        scratch_shapes=[
            pltpu.VMEM((2, KEY_BLOCKS * rows, HD), BF16),
            pltpu.VMEM((2, HD, KEY_BLOCKS * rows), BF16),
            pltpu.VMEM((2, HD, KEY_BLOCKS * rows), BF16),
            pltpu.VMEM((2, KEY_BLOCKS * rows, HD), F32),
        ],
        name="attention", compiler_params=params,
    )(lax.axis_index("ctx").reshape(1).astype(jnp.int32), local_memory(gathered), *prepared, out_grad[0], key_gain)
    returned = exchange(parts, "ctx", blocks, BACK_FIRST)
    grad_query = pl.pallas_call(
        query_end, out_shape=shape((rows, width), F32), name="query_end", compiler_params=params
    )(dq, query_raw[0], query_gain)
    gains = pl.pallas_call(
        near_sum, out_shape=near((others, 2, HD), BF16), name="near_sum", compiler_params=params
    )(local_memory(returned))
    gains = exchange(gains, ("head", "dp"), others, FAR_FIRST)
    grad_key, grad_value = pl.pallas_call(
        key_end,
        out_shape=(shape((rows, HD), F32), shape((rows, HD), F32)),
        name="key_end", compiler_params=params,
    )(local_memory(returned), key_raw[0], key_gain)
    pair_count = query_raw.shape[0] * rows * blocks * heads * others
    gains = pl.pallas_call(
        functools.partial(far_sum, factor=1.0 / math.sqrt(pair_count)),
        out_shape=shape((2, HD), F32),
        name="far_sum", compiler_params=params,
    )(local_memory(gains))
    return (grad_query[None], grad_key[None], grad_value[None], gains)


def solution(mesh):
    return jax.shard_map(
        local,
        mesh=mesh,
        in_specs=(
            P("dp", "ctx", "head"),
            P("dp", "ctx", "head"),
            P("dp", "ctx", "head"),
            P("dp", "ctx", "head"),
            P("dp", "ctx", "head"),
            P("dp", "head", "ctx"),
            P(),
            P(),
        ),
        out_specs=(P("dp", "ctx", "head"), P("dp", "ctx", "head"), P("dp", "ctx", "head"), P()),
        check_vma=False,
    )
```

```python
import functools
import math

import jax
import jax.numpy as jnp
from jax import lax
from jax.experimental import pallas as pl
from jax.experimental.pallas import tpu as pltpu
from jax.sharding import PartitionSpec as P

HD = 128
TAIL = 8
VMEM_LIMIT = 32 * 2**20
GATHER_FIRST = 10
GATHER_TURN = 3
BACK_FIRST = 14
BACK_TURN = 1
KEY_BLOCKS = 4
AHEAD = 1
Q_ROWS = 512
FAR_FIRST = 40
EPS = 1e-06
LOG2E = 1.4426950408889634
F32 = jnp.float32
BF16 = jnp.bfloat16


def prologue(q_ref, o_ref, g_ref, qgain_ref, qn_ref, qt_ref, gt_ref, delta_ref):
    rows = q_ref.shape[0]
    for h in range(q_ref.shape[1] // HD):
        cols = slice(h * HD, (h + 1) * HD)
        span = slice(h * rows, (h + 1) * rows)
        q = q_ref[:, cols].astype(F32)
        inverse = lax.rsqrt(jnp.mean(q * q, axis=-1, keepdims=True) + EPS)
        qn = (q * inverse * qgain_ref[...]).astype(BF16)
        qn_ref[span, :] = qn
        qt_ref[:, span] = qn.astype(F32).T.astype(BF16)
        g = g_ref[:, cols].astype(F32)
        gt_ref[:, span] = g.T.astype(BF16)
        delta = jnp.sum(g * o_ref[:, cols].astype(F32), axis=-1, keepdims=True)
        delta_ref[span, :] = jnp.broadcast_to(delta, (rows, HD))


def attention(
    block_ref, kv_ref, qn_ref, qt_ref, gt_ref, delta_ref, lt_ref, g_ref, q_ref, kgain_ref,
    dq_ref, parts_ref,
    kn_ref, kt_ref, vt_ref, unit_ref, lse_ref,
):
    blocks, rows = kv_ref.shape[0], kv_ref.shape[1] // 2
    width = qt_ref.shape[1]
    scale = 1.0 / math.sqrt(HD)
    pair = KEY_BLOCKS * rows
    twos = KEY_BLOCKS // 2
    wide = Q_ROWS
    block = block_ref[0]
    last = block // KEY_BLOCKS

    def prepare(j):
        ats = [(j * twos + i + GATHER_TURN) % (blocks // 2) for i in range(twos)]
        k = [kv_ref[pl.ds(2 * at, 2), :rows].reshape(2 * rows, HD) for at in ats]
        v = [kv_ref[pl.ds(2 * at, 2), rows:].reshape(2 * rows, HD) for at in ats]
        k = jnp.concatenate(k, axis=0).astype(F32)
        v = jnp.concatenate(v, axis=0).astype(F32)
        inverse = lax.rsqrt(jnp.mean(k * k, axis=-1, keepdims=True) + EPS)
        unit = k * inverse
        kn = (unit * kgain_ref[...]).astype(BF16)
        slot = j % 2
        unit_ref[slot] = unit
        kn_ref[slot] = kn
        kt_ref[slot] = kn.astype(F32).T.astype(BF16)
        vt_ref[slot] = v.T.astype(BF16)

    def step(j, k_gain, masked):
        slot = j % 2
        kn = kn_ref[slot]
        kt = kt_ref[slot]
        vt = vt_ref[slot]
        unit = unit_ref[slot]
        dkt = jnp.zeros((HD, pair), F32)
        dvt = jnp.zeros((HD, pair), F32)
        if masked:
            key_pos = j * pair + lax.broadcasted_iota(jnp.int32, (wide, pair), 1)
            query_pos = block * rows + lax.broadcasted_iota(jnp.int32, (wide, pair), 0) % rows
            keep = key_pos <= query_pos
        chunks = width // wide
        spans = [slice(c * wide, (c + 1) * wide) for c in range(chunks)]
        across = pair // HD

        def products(c):
            heads = range(c * wide // rows, (c + 1) * wide // rows)
            g = jnp.concatenate([g_ref[:, h * HD : (h + 1) * HD] for h in heads], axis=0)
            scores = jnp.dot(qn_ref[spans[c], :], kt, preferred_element_type=F32)
            return scores, jnp.dot(g, vt, preferred_element_type=F32)

        def weights(c, scores, dp):
            lse = jnp.concatenate([lse_ref[spans[c], :]] * across, axis=1)
            delta = jnp.concatenate([delta_ref[spans[c], :]] * across, axis=1)
            probs = jnp.exp2(scores * (scale * LOG2E) - lse)
            if masked:
                probs = jnp.where(keep, probs, 0.0)
            return probs.astype(BF16), (probs * (dp - delta)).astype(BF16)

        ahead = [products(c) for c in range(AHEAD)]
        for c in range(chunks):
            if c + AHEAD < chunks:
                ahead.append(products(c + AHEAD))
            low, ds = weights(c, *ahead[c])
            dvt += jnp.dot(gt_ref[:, spans[c]], low, preferred_element_type=F32)
            dkt += jnp.dot(qt_ref[:, spans[c]], ds, preferred_element_type=F32)
            dq_ref[spans[c], :] += jnp.dot(ds, kn, preferred_element_type=F32)
        dk = dkt.T * scale
        dv = dvt.T
        for i in range(twos):
            at = (j * twos + i + BACK_TURN) % (blocks // 2)
            piece = slice(2 * i * rows, 2 * (i + 1) * rows)
            parts_ref[pl.ds(2 * at, 2), :rows, :HD] = dk[piece].astype(BF16).reshape(2, rows, HD)
            parts_ref[pl.ds(2 * at, 2), :rows, HD:] = dv[piece].astype(BF16).reshape(2, rows, HD)
        if not masked:
            prepare(j + 1)
        return k_gain + jnp.sum(dk * unit, axis=0, keepdims=True)

    prepare(0)
    for h in range(width // rows):
        span = slice(h * rows, (h + 1) * rows)
        lse_ref[span, :] = jnp.broadcast_to(lt_ref[h : h + 1, :] * LOG2E, (HD, rows)).T
    dq_ref[...] = jnp.zeros(dq_ref.shape, F32)
    k_gain = lax.fori_loop(0, last, lambda j, s: step(j, s, False), jnp.zeros((1, HD), F32))
    k_gain = step(last, k_gain, True)

    def clear(j, carry):
        at = (j + BACK_TURN) % (blocks // 2)
        parts_ref[pl.ds(2 * at, 2), :rows] = jnp.zeros((2, rows, 2 * HD), BF16)
        return carry

    lax.fori_loop((last + 1) * twos, blocks // 2, clear, 0)
    product = jnp.zeros((rows, HD), F32)
    for h in range(width // rows):
        span = slice(h * rows, (h + 1) * rows)
        q = q_ref[:, h * HD : (h + 1) * HD].astype(F32)
        inverse = lax.rsqrt(jnp.mean(q * q, axis=-1, keepdims=True) + EPS)
        product += dq_ref[span, :] * (q * inverse)
    q_gain = jnp.sum(product, axis=0, keepdims=True) * scale
    sums = jnp.concatenate([q_gain, k_gain], axis=1)
    high = sums.astype(BF16).astype(F32)
    middle = (sums - high).astype(BF16).astype(F32)
    low = sums - high - middle
    tail = jnp.concatenate([high, middle, low, jnp.zeros((TAIL - 3, 2 * HD), F32)], axis=0)
    tail = tail.astype(BF16)
    for b in range(blocks):
        parts_ref[b, rows:] = tail


def query_end(dq_ref, q_ref, qgain_ref, gq_ref):
    rows = q_ref.shape[0]
    scale = 1.0 / math.sqrt(HD)
    for h in range(q_ref.shape[1] // HD):
        cols = slice(h * HD, (h + 1) * HD)
        grad_norm = dq_ref[h * rows : (h + 1) * rows, :] * scale
        q = q_ref[:, cols].astype(F32)
        inverse = lax.rsqrt(jnp.mean(q * q, axis=-1, keepdims=True) + EPS)
        unit = q * inverse
        grad_unit = grad_norm * qgain_ref[...]
        mean = jnp.mean(grad_unit * unit, axis=-1, keepdims=True)
        gq_ref[:, cols] = (grad_unit - unit * mean) * inverse


def near_sum(parts_ref, gains_ref):
    total = parts_ref[0, -TAIL:].astype(F32)
    for b in range(1, parts_ref.shape[0]):
        total += parts_ref[b, -TAIL:].astype(F32)
    sums = jnp.sum(total, axis=0, keepdims=True)
    sums = jnp.concatenate([sums[:, :HD], sums[:, HD:]], axis=0).astype(BF16)
    for i in range(gains_ref.shape[0]):
        gains_ref[i] = sums


def far_sum(gains_ref, out_ref, *, factor):
    out_ref[...] = jnp.sum(gains_ref[...].astype(F32), axis=0) * factor


def key_end(parts_ref, k_ref, kgain_ref, gk_ref, gv_ref):
    rows = k_ref.shape[0]
    total = parts_ref[0, :rows].astype(F32)
    for b in range(1, parts_ref.shape[0]):
        total += parts_ref[b, :rows].astype(F32)
    grad_norm = total[:, :HD]
    gv_ref[...] = total[:, HD:]
    k = k_ref[...].astype(F32)
    inverse = lax.rsqrt(jnp.mean(k * k, axis=-1, keepdims=True) + EPS)
    unit = k * inverse
    grad_unit = grad_norm * kgain_ref[...]
    mean = jnp.mean(grad_unit * unit, axis=-1, keepdims=True)
    gk_ref[...] = (grad_unit - unit * mean) * inverse


def local_memory(values):
    return pltpu.with_memory_space_constraint(values, pltpu.VMEM)


def exchange(values, axes, count, first):
    order = [[(first + i) % count for i in range(count)]]
    return lax.all_to_all(values, axes, 0, 0, axis_index_groups=order, tiled=True)


def local(query_raw, key_raw, value_rows, attn_out, out_grad, log_totals, query_gain, key_gain):
    blocks = lax.axis_size("ctx")
    rows, width = query_raw.shape[1], query_raw.shape[2]
    heads = width // HD
    others = lax.axis_size("head") * lax.axis_size("dp")
    shape = jax.ShapeDtypeStruct
    near = pltpu.VMEM
    params = pltpu.CompilerParams(vmem_limit_bytes=VMEM_LIMIT)
    in_vmem = pl.BlockSpec(memory_space=pltpu.VMEM)
    query_gain = query_gain.reshape(1, HD)
    key_gain = key_gain.reshape(1, HD)
    own = jnp.concatenate([key_raw[0], value_rows[0]], axis=0)
    spread = jnp.broadcast_to(own[None], (blocks, 2 * rows, HD))
    gathered = exchange(spread, "ctx", blocks, GATHER_FIRST)
    prepared = pl.pallas_call(
        prologue,
        out_shape=(
            near((heads * rows, HD), BF16),
            near((HD, heads * rows), BF16),
            near((HD, heads * rows), BF16),
            near((heads * rows, HD), F32),
        ),
        name="prologue", compiler_params=params,
    )(query_raw[0], attn_out[0], out_grad[0], query_gain)
    dq, parts = pl.pallas_call(
        attention,
        out_shape=(near((heads * rows, HD), F32), near((blocks, rows + TAIL, 2 * HD), BF16)),
        in_specs=[pl.BlockSpec(memory_space=pltpu.SMEM)] + [in_vmem] * 9,
        scratch_shapes=[
            pltpu.VMEM((2, KEY_BLOCKS * rows, HD), BF16),
            pltpu.VMEM((2, HD, KEY_BLOCKS * rows), BF16),
            pltpu.VMEM((2, HD, KEY_BLOCKS * rows), BF16),
            pltpu.VMEM((2, KEY_BLOCKS * rows, HD), F32),
            pltpu.VMEM((heads * rows, HD), F32),
        ],
        name="attention", compiler_params=params,
    )(lax.axis_index("ctx").reshape(1).astype(jnp.int32), local_memory(gathered), *prepared, log_totals[0], out_grad[0], query_raw[0], key_gain)
    returned = exchange(parts, "ctx", blocks, BACK_FIRST)
    grad_query = pl.pallas_call(
        query_end, out_shape=shape((rows, width), F32), name="query_end", compiler_params=params
    )(dq, query_raw[0], query_gain)
    gains = pl.pallas_call(
        near_sum, out_shape=near((others, 2, HD), BF16), name="near_sum", compiler_params=params
    )(local_memory(returned))
    gains = exchange(gains, ("head", "dp"), others, FAR_FIRST)
    grad_key, grad_value = pl.pallas_call(
        key_end,
        out_shape=(shape((rows, HD), F32), shape((rows, HD), F32)),
        name="key_end", compiler_params=params,
    )(local_memory(returned), key_raw[0], key_gain)
    pair_count = query_raw.shape[0] * rows * blocks * heads * others
    gains = pl.pallas_call(
        functools.partial(far_sum, factor=1.0 / math.sqrt(pair_count)),
        out_shape=shape((2, HD), F32),
        name="far_sum", compiler_params=params,
    )(local_memory(gains))
    return (grad_query[None], grad_key[None], grad_value[None], gains)


def solution(mesh):
    return jax.shard_map(
        local,
        mesh=mesh,
        in_specs=(
            P("dp", "ctx", "head"),
            P("dp", "ctx", "head"),
            P("dp", "ctx", "head"),
            P("dp", "ctx", "head"),
            P("dp", "ctx", "head"),
            P("dp", "head", "ctx"),
            P(),
            P(),
        ),
        out_specs=(P("dp", "ctx", "head"), P("dp", "ctx", "head"), P("dp", "ctx", "head"), P()),
        check_vma=False,
    )
```
